32 devices in a mesh: pos: 8 (over z, core), slab: 4 (over y, x).
Axes of the slice: x: 2, y: 2, z: 4, core: 2. Of those that a mesh axis runs over, the one named last changes fastest.
Arguments:
- probe: float32 [2, 256, 256], replicated, may hold values from -4 to 4
- object_slices: float32 [12, 2, 2048, 512], P('slab', None, 'pos')
- counts: int32 [4], P('slab'), may hold values from 1 to 3, as said below
- positions: int32 [32, 2], P('pos'), may hold values from 0 to 14, as said below
- amplitudes: float32 [32, 256, 256], P('pos'), may hold values from 0 to 2.5
Outputs:
- object_grad: float32 [12, 2, 2048, 512], P('slab', None, 'pos')
The draws below stay inside these ranges and needn't reach their ends.
Inputs may be any that keep to these rules, and one draw needn't show every extreme that they name: `counts`: every draw has a section with 3 slices in use and one with a single slice. positions p * 4 to p * 4 + 3 have tile rows p * 2 to p * 2 + 1 and never the object's last tile row; tile columns run from 0 to 2.
All inputs are finite; a program needn't handle non-finite values.
Results may differ from the reference program's by a relative error of at most 0.0003.
Values sent between devices are 32-bit elements; how exact they have to be, the bound alone decides.
No kernel may reach another device: no remote copies, remote signals or barrier semaphores. Data moves between devices by JAX's collectives and lax.ppermute only.
A program may use at most 128 MiB of HBM per device.

```python
import jax
import jax.numpy as jnp
from jax import lax

M = 256
POS_DEV = 4
SMAX = 3
TR_DEV = 2
GY = 4
TILE = 128
W = 512
BANDS = 8
SECTIONS = 4
ROWS = 2048
NPOS = 32
SLOTS = 12


def draw_object_slices(key, part):
    magnitude_key, phase_key = jax.random.split(jax.random.fold_in(key, 11))
    shape = (SLOTS, ROWS, W)
    magnitude = jax.random.uniform(magnitude_key, shape, jnp.float32, 0.96, 1.0)
    angles = jax.random.uniform(phase_key, shape, jnp.float32, -0.6, 0.6)
    return jnp.stack([magnitude * jnp.cos(angles), magnitude * jnp.sin(angles)], axis=1)


def draw_counts(key, part):
    drawn = jax.random.randint(jax.random.fold_in(key, 23), (SECTIONS,), 1, SMAX + 1)
    numbers = jnp.arange(SECTIONS)
    return jnp.where(numbers == 0, SMAX, jnp.where(numbers == 1, 1, drawn)).astype(jnp.int32)


def draw_positions(key, part):
    row_key, col_key = jax.random.split(jax.random.fold_in(key, 37))
    numbers = jnp.arange(NPOS)
    owners = numbers // POS_DEV
    reaches = jnp.where(owners == BANDS - 1, TR_DEV - 1, TR_DEV)
    offset = jax.random.randint(row_key, (NPOS,), 0, TR_DEV) % reaches
    offset = jnp.where(numbers == 0, 0, offset)
    row_tiles = owners * TR_DEV + offset
    col_tiles = jax.random.randint(col_key, (NPOS,), 0, GY - 1)
    col_tiles = jnp.where(numbers == 0, 0, col_tiles)
    return jnp.stack([row_tiles, col_tiles], axis=1).astype(jnp.int32)


def steps_of(stream_key, shape, cuts, least, largest):
    loudness, own = 1.0, jax.random.fold_in(stream_key, 6)
    for position, shards_of in cuts:
        steps = jnp.exp(jax.random.uniform(jax.random.fold_in(own, position), (shards_of,), jnp.float32, least / len(cuts), largest / len(cuts)))
        loudness = loudness * jnp.repeat(steps, shape[position] // shards_of).reshape([-1 if axis == position else 1 for axis in range(len(shape))])
    return loudness


def noise(own_key, shape, width, most, held_as=jnp.bfloat16):
    result = width * jax.random.normal(own_key, shape, jnp.float32)
    return jnp.clip(result, min=-most, max=most).astype(held_as)


def setup_inputs(seed: int = 0) -> dict:
    seeds = jax.random.split(jax.random.key(seed), 6)
    return {
        "probe": noise(seeds[0], (2, M, M), 1.0, 4.0, jnp.float32),
        "object_slices": draw_object_slices(jax.random.fold_in(seeds[5], 71), 0),
        "counts": draw_counts(jax.random.fold_in(seeds[5], 71), 0),
        "positions": draw_positions(jax.random.fold_in(seeds[5], 71), 0),
        "amplitudes": jnp.clip(2.5 * jax.random.uniform(seeds[4], (NPOS, M, M), jnp.float32) ** steps_of(seeds[4], (NPOS, M, M), ((0, 8),), -0.2, 0.2), 0.0, 2.5),
    }


FRESNEL = 20.0

def real_product(left, right):
    return jnp.dot(left, right, precision=lax.Precision.HIGHEST, preferred_element_type=jnp.float32)

def make_tables(extent):
    indices = jnp.arange(extent, dtype=jnp.int32)
    product = indices[:, None] * indices[None, :] % extent
    angles = product.astype(jnp.float32) * (2.0 * jnp.pi / extent)
    factor = 1.0 / jnp.sqrt(jnp.float32(extent))
    fourier_real = jnp.cos(angles) * factor
    fourier_imag = -jnp.sin(angles) * factor
    frequency = jnp.where(indices < extent // 2, indices, indices - extent).astype(jnp.float32) / extent
    phases = -2.0 * jnp.pi * FRESNEL * frequency * frequency
    kernel_real = jnp.cos(phases)
    kernel_imag = jnp.sin(phases)
    scaled_real = kernel_real[:, None] * fourier_real - kernel_imag[:, None] * fourier_imag
    scaled_imag = kernel_real[:, None] * fourier_imag + kernel_imag[:, None] * fourier_real
    highest = lax.Precision.HIGHEST
    propagator_real = jnp.dot(fourier_real.T, scaled_real, precision=highest) + jnp.dot(fourier_imag.T, scaled_imag, precision=highest)
    propagator_imag = jnp.dot(fourier_real.T, scaled_imag, precision=highest) - jnp.dot(fourier_imag.T, scaled_real, precision=highest)
    return ((fourier_real, fourier_imag), (propagator_real, propagator_imag))

def transform(matrix, signal):
    matrix_real, matrix_imag = matrix
    half_real = real_product(matrix_real, signal[0]) - real_product(matrix_imag, signal[1])
    half_imag = real_product(matrix_real, signal[1]) + real_product(matrix_imag, signal[0])
    out_real = real_product(half_real, matrix_real.T) - real_product(half_imag, matrix_imag.T)
    out_imag = real_product(half_real, matrix_imag.T) + real_product(half_imag, matrix_real.T)
    return jnp.stack([out_real, out_imag])

def complex_times(left_wave, right_wave):
    real_part = left_wave[0] * right_wave[0] - left_wave[1] * right_wave[1]
    imag_part = left_wave[0] * right_wave[1] + left_wave[1] * right_wave[0]
    return jnp.stack([real_part, imag_part])

def times_conjugate(left_wave, right_wave):
    real_part = left_wave[0] * right_wave[0] + left_wave[1] * right_wave[1]
    imag_part = left_wave[1] * right_wave[0] - left_wave[0] * right_wave[1]
    return jnp.stack([real_part, imag_part])

def far_field(fourier, fourier_conj, exit_wave, measured):
    spectrum = transform(fourier, exit_wave)
    modulus = jnp.sqrt(spectrum[0] * spectrum[0] + spectrum[1] * spectrum[1] + 1.0)
    residual = (1.0 - measured / modulus) * spectrum
    return transform(fourier_conj, residual)

def reference(probe, object_slices, counts, positions, amplitudes):
    fourier, propagator = make_tables(M)
    fourier_conj = (fourier[0], -fourier[1])
    prop_conj = (propagator[0], -propagator[1])
    slot_numbers = jnp.arange(SLOTS, dtype=jnp.int32)
    active = slot_numbers % SMAX < counts[slot_numbers // SMAX]
    anchor = jnp.zeros((), jnp.int32)
    float_type = object_slices.dtype
    wave_type = probe.dtype

    def one_position(summed_grad, inputs):
        corner, measured = inputs
        row_px = (corner[0] * TILE).astype(jnp.int32)
        col_px = (corner[1] * TILE).astype(jnp.int32)
        windows = lax.dynamic_slice(object_slices, (anchor, anchor, row_px, col_px), (SLOTS, 2, M, M))

        def step_forward(signal, entries):
            window, in_use = entries

            def advance(current_wave):
                passed = transform(propagator, current_wave).astype(float_type)
                return (complex_times(window, passed).astype(wave_type), passed)

            def unchanged(current_wave):
                return (current_wave, jnp.zeros((2, M, M), float_type))
            return lax.cond(in_use, advance, unchanged, signal)
        exit_wave, passed_all = lax.scan(step_forward, probe, (windows, active))
        seed_wave = far_field(fourier, fourier_conj, exit_wave, measured).astype(wave_type)

        def step_back(gradient, entries):
            window, passed, in_use = entries

            def advance(current_wave):
                patch_grad = times_conjugate(current_wave, passed).astype(float_type)
                inner_wave = times_conjugate(current_wave, window)
                return (transform(prop_conj, inner_wave).astype(wave_type), patch_grad)

            def unchanged(current_wave):
                return (current_wave, jnp.zeros((2, M, M), float_type))
            return lax.cond(in_use, advance, unchanged, gradient)
        unused, patches = lax.scan(step_back, seed_wave, (windows, passed_all, active), reverse=True)
        current = lax.dynamic_slice(summed_grad, (anchor, anchor, row_px, col_px), (SLOTS, 2, M, M))
        summed_grad = lax.dynamic_update_slice(summed_grad, current + patches, (anchor, anchor, row_px, col_px))
        return (summed_grad, None)
    object_grad, unused = lax.scan(one_position, jnp.zeros(object_slices.shape, float_type), (positions, amplitudes))
    return object_grad
```

```python
import jax
import jax.numpy as jnp
import numpy as np
from jax import lax
from jax.experimental import pallas as pl
from jax.experimental.pallas import tpu as pltpu
from jax.sharding import PartitionSpec as P

FRESNEL = 20.0

HBM = pl.BlockSpec(memory_space=pl.ANY)
VMEM = pl.BlockSpec(memory_space=pltpu.VMEM)
SMEM = pl.BlockSpec(memory_space=pltpu.SMEM)
BF16 = jnp.bfloat16
PARAMS = pltpu.CompilerParams(vmem_limit_bytes=48 * 2**20)


def real_form(m):
    return np.block([[m.real, -m.imag], [m.imag, m.real]])


def split_tables(n):
    half = n // 2
    i = np.arange(n)
    fourier = np.exp(-2j * np.pi * ((i[:, None] * i[None, :]) % n) / n) / np.sqrt(n)
    f = np.where(i < half, i, i - n) / n
    propagator = fourier.conj().T @ (np.exp(-2j * np.pi * FRESNEL * f * f)[:, None] * fourier)
    a, b = propagator[:half, :half], propagator[:half, half:]
    parts = [[(a + b) / 2, (a - b) / 2], [fourier[0::2, :half], fourier[1::2, :half]]]
    left = np.stack([np.stack([real_form(x) for x in pair]) for pair in parts])
    both = np.stack([left, np.swapaxes(left, -1, -2)], axis=1).astype(np.float32)
    high = both.astype(BF16)
    low = (both - high.astype(np.float32)).astype(BF16)
    return np.stack([high, low], axis=3)


def parity_table(n):
    half = n // 2
    table = np.zeros((n, n), np.float32)
    for i in range(n):
        table[i, (i % 2) * half + i // 2] = 1.0
    return np.stack([table, table.T]).astype(BF16)


def dot(a, b):
    return jnp.dot(a, b, preferred_element_type=jnp.float32)


def split(x):
    high = x.astype(BF16)
    return high, (x - high.astype(jnp.float32)).astype(BF16)


def fold(re, im):
    h = re.shape[0] // 2

    def cols(x):
        return jnp.concatenate([x[:, :h] + x[:, h:], x[:, :h] - x[:, h:]], axis=1)

    plus = jnp.concatenate([cols(re[:h] + re[h:]), cols(im[:h] + im[h:])], axis=0)
    minus = jnp.concatenate([cols(re[:h] - re[h:]), cols(im[:h] - im[h:])], axis=0)
    return plus, minus


def products(z, tab, op, side):
    h = z[0].shape[0] // 2
    u = []
    for s in range(2):
        zh, zl = split(z[s])
        lh, ll = tab[op, side, s, 0], tab[op, side, s, 1]
        u.append(dot(lh, zh) + dot(ll, zh) + dot(lh, zl))
    v = []
    for t in range(2):
        c = slice(t * h, (t + 1) * h)
        rows = [jnp.concatenate([u[s][:h, c], u[s][h:, c]], axis=1) for s in range(2)]
        ah, al = split(jnp.concatenate(rows, axis=0))
        rh, rl = tab[op, 1 - side, t, 0], tab[op, 1 - side, t, 1]
        v.append(dot(ah, rh) + dot(al, rh) + dot(ah, rl))
    return v


def unfold(v):
    h = v[0].shape[0] // 2

    def plane(c):
        a, b = v[0][:, c], v[1][:, c]
        x = jnp.concatenate([a + b, a - b], axis=1)
        return jnp.concatenate([x[:h] + x[h:], x[:h] - x[h:]], axis=0)

    return plane(slice(0, h)), plane(slice(h, 2 * h))


def transform(re, im, tab, op, side):
    return unfold(products(fold(re, im), tab, op, side))


def far_field(re, im, measured, tab):
    h = re.shape[0] // 2
    v = products(fold(re, im), tab, 1, 0)
    r = []
    for t in range(2):
        sr, si = v[t][:, :h], v[t][:, h:]
        modulus = jnp.sqrt(sr * sr + si * si + 1.0)
        scale = 1.0 - measured[:, t * h : (t + 1) * h] / modulus
        r.append((sr * scale, si * scale))
    z = []
    for s in range(2):
        rows = slice(s * h, (s + 1) * h)
        planes = [jnp.concatenate([r[0][c][rows], r[1][c][rows]], axis=1) for c in range(2)]
        z.append(jnp.concatenate(planes, axis=0))
    return unfold(products(z, tab, 1, 1))


def place(info, pos, j):
    off = pos[j, 0] - info[5]
    return off, pl.multiple_of(pos[j, 1] * info[6], 128)


def window_copies(band, rims, k, off, col, buf, sem, tile, go, out=False):
    rows_in_band = band.shape[2]
    m = 2 * tile

    def run(outer, inner, which):
        src, dst = (inner, outer) if out else (outer, inner)
        go(pltpu.make_async_copy(src, dst, sem.at[which]))

    top = pl.multiple_of(off * tile, tile)
    run(band.at[k, :, pl.ds(top, tile), pl.ds(col, m)], buf.at[:, pl.ds(0, tile), :], 0)
    inside = (off + 2) * tile <= rows_in_band

    @pl.when(inside)
    def _():
        low = pl.multiple_of(jnp.minimum(off + 1, rows_in_band // tile - 1) * tile, tile)
        run(band.at[k, :, pl.ds(low, tile), pl.ds(col, m)], buf.at[:, pl.ds(tile, tile), :], 1)

    @pl.when(jnp.logical_not(inside))
    def _():
        run(rims[k].at[:, :, pl.ds(col, m)], buf.at[:, pl.ds(tile, tile), :], 1)


def start(copy):
    copy.start()


def wait(copy):
    copy.wait()


def prep_kernel(info, probe, amps, tab, parity, psi0, sorted_amps):
    @pl.when(info[3] == 1)
    def _():
        re, im = transform(probe[0], probe[1], tab, 0, 0)
        psi0[0] = re
        psi0[1] = im

    @pl.when(info[4] == 1)
    def _():
        def body(j, carry):
            def exact(left, right, left_is_table):
                x = right if left_is_table else left
                high, rest = split(x)
                low = (x - high.astype(jnp.float32) - rest.astype(jnp.float32)).astype(BF16)
                terms = [high, rest, low]
                if left_is_table:
                    return sum(dot(left, y) for y in terms)
                return sum(dot(y, right) for y in terms)

            sorted_amps[j] = exact(parity[1], exact(amps[j], parity[0], False), True)
            return carry

        lax.fori_loop(0, amps.shape[0], body, 0)


def feed_kernel(tile, npos, info, pos, band, rim, *rest):
    outs, sem = rest[:npos], rest[npos]

    @pl.when(info[0] == 0)
    def _():
        for go in (start, wait):
            for j in range(npos):
                off, col = place(info, pos, j)
                window_copies(band, [rim], 0, off, col, outs[j], sem.at[j], tile, go)


def feed_more_kernel(tile, npos, slots, info, pos, band, *rest):
    rims, out, sem = rest[:slots], rest[slots], rest[slots + 1]

    @pl.when(info[0] == 0)
    def _():
        for go in (start, wait):
            for j in range(npos):
                off, col = place(info, pos, j)
                for k in range(1, slots):
                    window_copies(
                        band, rims, k, off, col, out.at[j, k - 1], sem.at[j, k], tile, go
                    )


def load_windows(info, j, off, col, band, rims, shipped, shipped_more, win, sem, tile, go):
    count, extra, slots = info[1], info[2], len(rims)
    for k in range(slots):

        @pl.when(k < count)
        def _():
            window_copies(band, rims, k, off, col, win.at[k], sem.at[k], tile, go)

    @pl.when(extra > 0)
    def _():
        go(pltpu.make_async_copy(shipped, win.at[count], sem.at[count, 0]))

    for k in range(1, slots):

        @pl.when(k < extra)
        def _():
            go(
                pltpu.make_async_copy(
                    shipped_more.at[j, k - 1], win.at[count + k], sem.at[count + k, 0]
                )
            )


def forward_kernel(tile, npos, slots, *refs):
    (tick, info, pos, wave, shipped, shipped_more, band) = refs[:7]
    rims = refs[7 : 7 + slots]
    (psi0, amps, tab, _, out, stored, win, psi, x, amp, wsem, psem, asem) = refs[7 + slots :]
    j = tick[0] - info[0]
    first, last = info[3], info[4]
    total = info[1] + info[2]

    @pl.when((j >= 0) & (j < npos) & (info[0] > 0))
    def _():
        off, col = place(info, pos, j)
        args = (info, j, off, col, band, rims, shipped, shipped_more, win, wsem, tile)
        load_windows(*args, start)

        @pl.when(last == 1)
        def _():
            pltpu.make_async_copy(amps.at[j], amp, asem).start()

        x[...] = wave[...]
        load_windows(*args, wait)

        def step(q, carry):
            known = (first == 1) & (q == 0)

            @pl.when(known)
            def _():
                psi[q] = psi0[...]

            @pl.when(jnp.logical_not(known))
            def _():
                re, im = transform(x[0], x[1], tab, 0, 0)
                psi[q, 0] = re
                psi[q, 1] = im

            pltpu.make_async_copy(psi.at[q], stored.at[j, q], psem.at[q]).start()
            pr, pi = psi[q, 0], psi[q, 1]
            wr, wi = win[q, 0], win[q, 1]
            x[0] = wr * pr - wi * pi
            x[1] = wr * pi + wi * pr
            return carry

        lax.fori_loop(0, total, step, 0)

        @pl.when(last == 1)
        def _():
            pltpu.make_async_copy(amps.at[j], amp, asem).wait()
            re, im = far_field(x[0], x[1], amp[...], tab)
            out[0] = re
            out[1] = im

        @pl.when(last == 0)
        def _():
            out[...] = x[...]

        def drain(q, carry):
            pltpu.make_async_copy(psi.at[q], stored.at[j, q], psem.at[q]).wait()
            return carry

        lax.fori_loop(0, total, drain, 0)


def backward_kernel(tile, npos, slots, stages, *refs):
    (tick, info, pos, gin, seed, shipped, shipped_more, band) = refs[:8]
    rims = refs[8 : 8 + slots]
    refs = refs[8 + slots :]
    stored, tab = refs[:2]
    refs = refs[2 + slots + 2 :]
    out, sums = refs[:2]
    sum_rims = refs[2 : 2 + slots]
    more, win, psi, total, g, wsem, psem, tsem, msem = refs[2 + slots :]
    j = tick[0] - 2 * stages + info[0]
    count, extra, first, last = info[1], info[2], info[3], info[4]
    live = (j >= 0) & (j < npos)

    @pl.when(live & (info[0] > 0))
    def _():
        off, col = place(info, pos, j)
        args = (info, j, off, col, band, rims, shipped, shipped_more, win, wsem, tile)
        load_windows(*args, start)
        number = count + extra

        def psi_copy(q):
            return pltpu.make_async_copy(stored.at[j, q], psi.at[q], psem.at[q])

        def each(go):
            def body(q, carry):
                go(psi_copy(q))
                return carry

            lax.fori_loop(0, number, body, 0)

        each(start)

        def sum_copies(k, go, back):
            window_copies(
                sums, sum_rims, k, off, col, total.at[k], tsem.at[k], tile, go, out=back
            )

        for k in range(slots):

            @pl.when(k < count)
            def _():
                sum_copies(k, start, False)

        @pl.when(last == 1)
        def _():
            g[...] = seed[...]

        @pl.when(last == 0)
        def _():
            g[...] = gin[...]

        load_windows(*args, wait)
        each(wait)
        for k in range(slots):

            @pl.when(k < count)
            def _():
                sum_copies(k, wait, False)

        def step(i, carry):
            q = number - 1 - i
            gr, gi = g[0], g[1]
            pr, pi = psi[q, 0], psi[q, 1]
            dr = gr * pr + gi * pi
            di = gi * pr - gr * pi

            @pl.when(q < count)
            def _():
                total[q, 0] = total[q, 0] + dr
                total[q, 1] = total[q, 1] + di

            @pl.when(q == count)
            def _():
                out[0] = dr
                out[1] = di

            @pl.when(q > count)
            def _():
                psi[q, 0] = dr
                psi[q, 1] = di
                pltpu.make_async_copy(
                    psi.at[q], more.at[j, q - count - 1], msem.at[q - count - 1]
                ).start()

            @pl.when(jnp.logical_not((first == 1) & (q == 0)))
            def _():
                wr, wi = win[q, 0], win[q, 1]
                re, im = transform(gr * wr + gi * wi, gi * wr - gr * wi, tab, 0, 1)
                g[0] = re
                g[1] = im

            return carry

        lax.fori_loop(0, number, step, 0)

        @pl.when(first == 0)
        def _():
            out[...] = g[...]

        for go in (start, wait):
            for k in range(slots):

                @pl.when(k < count)
                def _():
                    sum_copies(k, go, True)

        for k in range(1, slots):

            @pl.when(k < extra)
            def _():
                pltpu.make_async_copy(
                    psi.at[count + k], more.at[j, k - 1], msem.at[k - 1]
                ).wait()

    @pl.when(live & (info[0] == 0))
    def _():
        off, col = place(info, pos, j)

        def both(go, back):
            window_copies(
                sums, sum_rims, 0, off, col, total.at[0], tsem.at[0], tile, go, out=back
            )

        both(start, False)
        both(wait, False)
        total[0] = total[0] + gin[...]
        both(start, True)
        both(wait, True)


def more_sums_kernel(tile, npos, slots, *refs):
    (info, pos, arrived) = refs[:3]
    refs = refs[3 + slots + 1 :]
    sums = refs[0]
    sum_rims = refs[1 : 1 + slots]
    total, patch, tsem, psem = refs[1 + slots :]

    @pl.when(info[0] == 0)
    def _():
        for j in range(npos):
            off, col = place(info, pos, j)
            for k in range(1, slots):

                @pl.when(k < info[1])
                def _():
                    def both(go, back):
                        window_copies(
                            sums, sum_rims, k, off, col, total, tsem, tile, go, out=back
                        )

                    copy = pltpu.make_async_copy(arrived.at[j, k - 1], patch, psem)
                    copy.start()
                    both(start, False)
                    both(wait, False)
                    copy.wait()
                    total[...] = total[...] + patch[...]
                    both(start, True)
                    both(wait, True)


def on_device(probe, object_slices, counts, positions, amplitudes):
    f32 = jnp.float32
    m = probe.shape[1]
    tile = m // 2
    slots, _, band_rows, columns = object_slices.shape
    npos = positions.shape[0]
    segments = lax.axis_size("slab")
    bands = lax.axis_size("pos")
    me = lax.axis_index("slab")
    stages = segments - 1
    wave_shape = jax.ShapeDtypeStruct((2, m, m), f32)
    more_shape = jax.ShapeDtypeStruct((npos, max(slots - 1, 1), 2, m, m), f32)
    store_shape = jax.ShapeDtypeStruct((npos, 2 * slots, 2, m, m), f32)
    sums_shape = jax.ShapeDtypeStruct((slots, 2, band_rows, columns), f32)
    rim_shape = jax.ShapeDtypeStruct((2, tile, columns), f32)

    def call(kernel, out_shape, in_specs, out_specs, scratch=(), aliases=None):
        return pl.pallas_call(
            kernel,
            out_shape=out_shape,
            in_specs=in_specs,
            out_specs=out_specs,
            scratch_shapes=list(scratch),
            input_output_aliases=aliases or {},
            compiler_params=PARAMS,
        )

    order = [1, 0] + list(range(2, segments))
    onward = [(order[i], order[i + 1]) for i in range(segments - 1)]
    wave_pairs = onward[1:]
    back_pairs = [(b, a) for a, b in onward]

    second = jnp.where(me == 1, counts, 0)
    known = 1
    while known < segments:
        pairs = [(order[i], order[i + known]) for i in range(min(known, segments - known))]
        second = second + lax.ppermute(second, "slab", pairs)
        known *= 2

    stage = jnp.where(me == 0, 1, jnp.where(me == 1, 0, me)).astype(jnp.int32)
    first = (me == 0).astype(jnp.int32)
    last = (stage == stages).astype(jnp.int32)
    band_start = (lax.axis_index("pos") * (band_rows // tile)).astype(jnp.int32)
    here = counts[0]
    plain = jnp.stack([stage, here, here * 0, first, last, band_start, jnp.int32(tile)])
    info = plain.at[2].set(first * second[0])

    up = [(i, i - 1) for i in range(1, bands)]
    down = [(i, i + 1) for i in range(bands - 1)]
    rims = [lax.ppermute(object_slices[k, :, :tile, :], "pos", up) for k in range(slots)]

    fed = call(
        lambda *r: feed_kernel(tile, npos, *r),
        [wave_shape] * npos,
        [SMEM, SMEM, HBM, HBM],
        [HBM] * npos,
        [pltpu.SemaphoreType.DMA((npos, 2))],
    )(plain, positions, object_slices, rims[0])
    shipped = [lax.ppermute(w, "slab", onward[:1]) for w in fed]

    def nothing(shape):
        return call(lambda *r: None, shape, [SMEM], HBM)(plain)

    def ship_more():
        more = call(
            lambda *r: feed_more_kernel(tile, npos, slots, *r),
            more_shape,
            [SMEM, SMEM, HBM] + [HBM] * slots,
            HBM,
            [pltpu.SemaphoreType.DMA((npos, slots, 2))],
        )(plain, positions, object_slices, *rims)
        return lax.ppermute(more, "slab", onward[:1])

    several = second[0] > 1
    shipped_more = lax.cond(several, ship_more, lambda: nothing(more_shape))

    tab = jnp.asarray(split_tables(m))
    psi0, amps = call(
        prep_kernel,
        [wave_shape, jax.ShapeDtypeStruct((npos, m, m), f32)],
        [SMEM, VMEM, VMEM, VMEM, VMEM],
        [VMEM, VMEM],
    )(plain, probe, amplitudes, tab, jnp.asarray(parity_table(m)))

    dma = pltpu.SemaphoreType.DMA
    big = 2 * slots
    forward_call = call(
        lambda *r: forward_kernel(tile, npos, slots, *r),
        [wave_shape, store_shape],
        [SMEM, SMEM, SMEM, VMEM, HBM, HBM, HBM] + [HBM] * slots + [VMEM, HBM, VMEM, HBM],
        [VMEM, HBM],
        [
            pltpu.VMEM((big, 2, m, m), f32),
            pltpu.VMEM((big, 2, m, m), f32),
            pltpu.VMEM((2, m, m), f32),
            pltpu.VMEM((m, m), f32),
            dma((big, 2)),
            dma((big,)),
            dma(()),
        ],
        {10 + slots: 1},
    )
    base = 8 + slots + 2
    aliases = {base: 1}
    aliases.update({base + 1 + k: 2 + k for k in range(slots)})
    aliases[base + 1 + slots] = 2 + slots
    backward_call = call(
        lambda *r: backward_kernel(tile, npos, slots, stages, *r),
        [wave_shape, sums_shape] + [rim_shape] * slots + [more_shape],
        [SMEM] * 3
        + [VMEM, VMEM, HBM, HBM, HBM]
        + [HBM] * slots
        + [HBM, VMEM]
        + [HBM] * (slots + 2),
        [VMEM] + [HBM] * (slots + 2),
        [
            pltpu.VMEM((big, 2, m, m), f32),
            pltpu.VMEM((big, 2, m, m), f32),
            pltpu.VMEM((slots, 2, m, m), f32),
            pltpu.VMEM((2, m, m), f32),
            dma((big, 2)),
            dma((big,)),
            dma((slots, 2)),
            dma((slots,)),
        ],
        aliases,
    )

    def forward(t, state, window):
        tick = jnp.full((1,), t, jnp.int32)
        return forward_call(
            tick, info, positions, state["wave"], window, shipped_more,
            object_slices, *rims, psi0, amps, tab, state["stored"],
        )

    def backward(t, state, window, seed):
        tick = jnp.full((1,), t, jnp.int32)
        result = backward_call(
            tick, info, positions, state["grad"], seed, window, shipped_more,
            object_slices, *rims, state["stored"], tab[:1],
            state["sums"], *state["sum_rims"], state["more"],
        )
        return result[0], result[1], list(result[2 : 2 + slots]), result[2 + slots]

    empty = jnp.zeros((2, m, m), f32)
    state = {
        "wave": empty,
        "grad": empty,
        "stored": nothing(store_shape),
        "sums": jnp.zeros(sums_shape.shape, f32),
        "sum_rims": [jnp.zeros(rim_shape.shape, f32) + k * 0.0 for k in range(slots)],
        "more": nothing(more_shape),
    }
    ticks = 2 * stages + npos

    def turn(t, state, window_f, window_b, do_f, send_f, do_b, send_b):
        state = dict(state)
        seed = state["wave"]
        if do_f:
            seed, state["stored"] = forward(t, state, window_f)
            if send_f and wave_pairs:
                state["wave"] = lax.ppermute(seed, "slab", wave_pairs)
        if do_b:
            grad, state["sums"], state["sum_rims"], state["more"] = backward(
                t, state, window_b, seed
            )
            if send_b:
                state["grad"] = lax.ppermute(grad, "slab", back_pairs)
        return state

    if ticks <= 16:
        for t in range(1, ticks):
            state = turn(
                t,
                state,
                shipped[min(max(t - 1, 0), npos - 1)],
                shipped[min(max(t - 2 * stages + 1, 0), npos - 1)],
                t < stages + npos,
                t < stages + npos - 1,
                t >= stages,
                t < ticks - 1,
            )
    else:
        every = jnp.stack(shipped)

        def body(t, state):
            now = every[jnp.clip(t - 1, 0, npos - 1)]
            then = every[jnp.clip(t - 2 * stages + 1, 0, npos - 1)]
            return turn(t, state, now, then, True, True, True, True)

        state = lax.fori_loop(1, ticks, body, state)

    sums, sum_rims, more = state["sums"], state["sum_rims"], state["more"]

    def add_more(sums, sum_rims, more):
        arrived = lax.ppermute(more, "slab", [(0, 1)])
        result = call(
            lambda *r: more_sums_kernel(tile, npos, slots, *r),
            [sums_shape] + [rim_shape] * slots,
            [SMEM, SMEM, HBM] + [HBM] * (slots + 1),
            [HBM] * (slots + 1),
            [
                pltpu.VMEM((2, m, m), f32),
                pltpu.VMEM((2, m, m), f32),
                dma((2,)),
                dma(()),
            ],
            {3 + k: k for k in range(slots + 1)},
        )(plain, positions, arrived, sums, *sum_rims)
        return result[0], list(result[1:])

    sums, sum_rims = lax.cond(
        several, add_more, lambda a, b, c: (a, b), sums, sum_rims, more
    )
    spilled = jnp.stack([lax.ppermute(r, "pos", down) for r in sum_rims])
    return sums.at[:, :, :tile, :].add(spilled)


def solution(mesh):
    placed = (P(), P("slab", None, "pos", None), P("slab"), P("pos", None), P("pos", None, None))
    return jax.shard_map(
        on_device,
        mesh=mesh,
        in_specs=placed,
        out_specs=P("slab", None, "pos", None),
        check_vma=False,
    )
```
